32 devices in a mesh: groups: 2 (over x), section: 16 (over z, y, core).
Axes of the slice: x: 2, y: 2, z: 4, core: 2. Of those that a mesh axis runs over, the one named last changes fastest.
Arguments:
- queries: bfloat16 [4096, 4096], P(('groups', 'section')), parts along dimension 0, may hold values from -9 to 9
- slice_keys: bfloat16 [4096, 512], P(('groups', 'section')), parts along dimension 0, may hold values from -6 to 6
- slice_values: bfloat16 [4096, 512], P(('groups', 'section')), parts along dimension 0, may hold values from -6 to 6
- cache_keys: bfloat16 [12288, 512], P(('groups', 'section')), parts along dimension 0, may hold values from -250 to 250
- cache_values: bfloat16 [12288, 512], P(('groups', 'section')), parts along dimension 0, may hold values from -6 to 6
- lent_keys: bfloat16 [32, 3, 1024, 512], P(('groups', 'section')), parts along dimension 0, may hold values from -6 to 6
- lent_values: bfloat16 [32, 3, 1024, 512], P(('groups', 'section')), parts along dimension 0, may hold values from -6 to 6
- lent_len: int32 [32, 3], P(('groups', 'section')), parts along dimension 0, may hold values from 1 to 1024
- slice_index: int32 [32], P(('groups', 'section')), parts along dimension 0, may hold values from 1 to 3
- lend_block: int32 [2, 32, 3], P(None, ('groups', 'section')), parts along dimension 1, may hold values from 0 to 1
- sinks: float32 [64], replicated, may hold values from -1 to 4
- gain: float32 [4096], replicated, may hold values from 0.5 to 2
Outputs:
- first_output: bfloat16 [4096, 4096], P(('groups', 'section')), parts along dimension 0
- second_output: bfloat16 [4096, 4096], P(('groups', 'section')), parts along dimension 0
The draws below stay inside these ranges and needn't reach their ends.
There are 2 independent parts, one for each index of `groups`. The reference program is written for one: setup_inputs(seed, part) draws one part's arguments, and reference() takes and returns one part's arrays. A program takes and returns all parts, laid end to end along the dimension named above; an argument that names none is the same for every part. Nothing has to cross between parts.
All inputs are finite; a program needn't handle non-finite values.
Results may differ from the reference program's by a relative error of at most 0.011.
Values may be sent and summed in bfloat16 or wider, within the bound.
A program may use at most 128 MiB of HBM per device.

```python
import math
import jax
import jax.numpy as jnp
from jax import lax

QUERY_HEADS = 64
KEY_VALUE_HEADS = 8
HEAD_SIZE = 64
SLICE = 128
QB = 64
CACHE_SLICES = 3
LROWS = 1024
REACH = 3
STEPS = 2
SECTIONS = 16
CACHE = 384
QW = 4096
KVW = 512


def draw_cache_keys(key, part):
    base = jnp.clip(jax.random.normal(key, (SECTIONS, CACHE, KVW), jnp.float32), -6.0, 6.0)
    return base.reshape(SECTIONS * CACHE, KVW).astype(jnp.bfloat16)


def set_ends(result, key, least, top_value):
    longest = result.shape.index(max(result.shape))
    spots = []
    for shift in (0, 1):
        where = [jax.random.randint(jax.random.fold_in(key, axis), (), 0, length) for axis, length in enumerate(result.shape)]
        where[longest] = (where[longest] + shift) % result.shape[longest]
        spots.append(tuple(where))
    return result.at[spots[0]].set(least).at[spots[1]].set(top_value)


def levels(rng, extent, cuts, smallest, largest):
    def one(axis_at, shards_of):
        draws = jax.random.uniform(jax.random.fold_in(jax.random.fold_in(rng, 6), axis_at), (shards_of,), jnp.float32, smallest / len(cuts), largest / len(cuts))
        return jnp.repeat(jnp.exp(draws), extent[axis_at] // shards_of).reshape((-1,) + (1,) * (len(extent) - axis_at - 1))

    level = one(*cuts[0])
    for cut in cuts[1:]:
        level = level * one(*cut)
    return level


def bell_draw(rng, dims, deviation, most, split=(), kind=jnp.bfloat16):
    level = levels(rng, dims, split, -0.22, 0.18) if split else 1.0
    entries = jax.random.normal(rng, dims, jnp.float32) * deviation * level
    return jnp.minimum(jnp.maximum(entries, -most), most).astype(kind)


def setup_inputs(seed: int = 0, part: int = 0) -> dict:
    splits = jax.random.split(jax.random.key(seed), 13)
    part_keys = jax.random.split(jax.random.fold_in(splits[12], part), 13)
    queries = bell_draw(part_keys[0], (SECTIONS * SLICE, QW), 1.5, 9.0, ((0, 16),))
    slice_keys = bell_draw(part_keys[1], (SECTIONS * SLICE, KVW), 1.0, 6.0, ((0, 16),))
    slice_values = bell_draw(part_keys[2], (SECTIONS * SLICE, KVW), 1.0, 6.0, ((0, 16),))
    cache_keys = draw_cache_keys(jax.random.fold_in(jax.random.fold_in(splits[12], part), 71), part)
    cache_values = bell_draw(part_keys[4], (SECTIONS * CACHE, KVW), 1.0, 6.0, ((0, 16),))
    lent_keys = bell_draw(part_keys[5], (SECTIONS, REACH, LROWS, KVW), 1.0, 6.0, ((0, 16),))
    lent_values = bell_draw(part_keys[6], (SECTIONS, REACH, LROWS, KVW), 1.0, 6.0, ((0, 16),))
    lent_len = set_ends(jax.random.randint(part_keys[7], (SECTIONS, REACH), 1, LROWS + 1), jax.random.fold_in(part_keys[7], 1), 1, LROWS).astype(jnp.int32)
    slice_index = set_ends(jax.random.randint(part_keys[8], (SECTIONS,), 1, CACHE_SLICES + 1), jax.random.fold_in(part_keys[8], 1), 1, CACHE_SLICES).astype(jnp.int32)
    lend_block = set_ends(jax.random.randint(part_keys[9], (STEPS, SECTIONS, REACH), 0, SLICE // QB), jax.random.fold_in(part_keys[9], 1), 0, (SLICE // QB) - 1).astype(jnp.int32)
    sinks = jnp.clip(jax.random.uniform(splits[10], (QUERY_HEADS,), jnp.float32, -1.0, 4.0), -1.0, 4.0)
    gain = jnp.clip(jnp.exp(jax.random.uniform(splits[11], (QW,), jnp.float32, math.log(0.5), math.log(2.0))), 0.5, 2.0)
    return {"queries": queries, "slice_keys": slice_keys, "slice_values": slice_values, "cache_keys": cache_keys, "cache_values": cache_values, "lent_keys": lent_keys, "lent_values": lent_values, "lent_len": lent_len, "slice_index": slice_index, "lend_block": lend_block, "sinks": sinks, "gain": gain}


def group_terms(query_matrix, key_rows, value_rows, valid):
    row_count = query_matrix.shape[0]
    group_width = QUERY_HEADS // KEY_VALUE_HEADS
    query_heads = query_matrix.reshape(row_count, KEY_VALUE_HEADS, group_width, HEAD_SIZE).astype(jnp.float32)
    key_heads = key_rows.reshape(-1, KEY_VALUE_HEADS, HEAD_SIZE).astype(jnp.float32)
    value_heads = value_rows.reshape(-1, KEY_VALUE_HEADS, HEAD_SIZE).astype(jnp.float32)
    score = jnp.einsum('rhgd,khd->hgrk', query_heads, key_heads, precision=lax.Precision.HIGHEST) * HEAD_SIZE ** (-0.5)
    score = jnp.where(valid[None, None], score, -jnp.inf)
    peak = lax.optimization_barrier(jnp.max(score, axis=-1))
    weight = jnp.exp(score - peak[..., None])
    total = lax.optimization_barrier(jnp.sum(weight, axis=-1))
    rounded = lax.optimization_barrier(weight.astype(jnp.bfloat16)).astype(jnp.float32)
    summed = jnp.einsum('hgrk,khd->hgrd', rounded, value_heads, precision=lax.Precision.HIGHEST)
    return (peak, total, summed)

def widen(terms, start, row_count):
    peak, total, summed = terms
    full_peak = jnp.full(peak.shape[:2] + (row_count,), -jnp.inf, jnp.float32)
    full_total = jnp.zeros(peak.shape[:2] + (row_count,), jnp.float32)
    full_summed = jnp.zeros(peak.shape[:2] + (row_count, summed.shape[3]), jnp.float32)
    full_peak = lax.dynamic_update_slice_in_dim(full_peak, peak, start, 2)
    full_total = lax.dynamic_update_slice_in_dim(full_total, total, start, 2)
    full_summed = lax.dynamic_update_slice_in_dim(full_summed, summed, start, 2)
    return (full_peak, full_total, full_summed)

def combine(parts, sinks, row_count):
    peaks = jnp.stack([part[0] for part in parts])
    totals = jnp.stack([part[1] for part in parts])
    summeds = jnp.stack([part[2] for part in parts])
    sink_logit = sinks.reshape(KEY_VALUE_HEADS, QUERY_HEADS // KEY_VALUE_HEADS)[:, :, None]
    top = jnp.maximum(lax.optimization_barrier(jnp.max(peaks, axis=0)), sink_logit)
    factor = jnp.exp(peaks - top)
    denom = lax.optimization_barrier(jnp.sum(totals * factor, axis=0)) + jnp.exp(sink_logit - top)
    out = lax.optimization_barrier(jnp.sum(summeds * factor[..., None], axis=0)) / denom[..., None]
    return out.transpose(2, 0, 1, 3).reshape(row_count, QUERY_HEADS * HEAD_SIZE)

def attend(query_all, key_all, value_all, cache_k, cache_v, lent_keys, lent_values, lent_len, slice_index, plan, sinks):
    position = jnp.arange(SLICE, dtype=jnp.int32)
    slice_valid = position[None, :] <= position[:, None]
    cache_pos = jnp.arange(CACHE, dtype=jnp.int32)
    lent_pos = jnp.arange(LROWS, dtype=jnp.int32)

    def one_section(section_id):
        current = query_all[section_id]
        key_rows = jnp.concatenate([cache_k[section_id], key_all[section_id]], axis=0)
        value_rows = jnp.concatenate([cache_v[section_id], value_all[section_id]], axis=0)
        own_rows = slice_index[section_id] * SLICE
        cache_valid = jnp.broadcast_to(cache_pos[None, :] < own_rows, (SLICE, CACHE))
        valid = jnp.concatenate([cache_valid, slice_valid], axis=1)
        parts = [group_terms(current, key_rows, value_rows, valid)]
        for dist in range(REACH):
            target = ((section_id + dist + 1) % SECTIONS).astype(jnp.int32)
            start = (plan[section_id, dist] * QB).astype(jnp.int32)
            block = lax.dynamic_slice_in_dim(current, start, QB, 0)
            lent_valid = jnp.broadcast_to(lent_pos[None, :] < lent_len[target, dist], (QB, LROWS))
            terms = group_terms(block, lent_keys[target, dist], lent_values[target, dist], lent_valid)
            parts.append(widen(terms, start, SLICE))
        return combine(parts, sinks, SLICE)
    return lax.map(one_section, jnp.arange(SECTIONS, dtype=jnp.int32))

def reference(queries, slice_keys, slice_values, cache_keys, cache_values, lent_keys, lent_values, lent_len, slice_index, lend_block, sinks, gain):
    query_all = queries.reshape(SECTIONS, SLICE, QW)
    key_all = slice_keys.reshape(SECTIONS, SLICE, KVW)
    value_all = slice_values.reshape(SECTIONS, SLICE, KVW)
    cache_k = cache_keys.reshape(SECTIONS, CACHE, KVW)
    cache_v = cache_values.reshape(SECTIONS, CACHE, KVW)
    first = attend(query_all, key_all, value_all, cache_k, cache_v, lent_keys, lent_values, lent_len, slice_index, lend_block[0], sinks).astype(jnp.bfloat16)
    stream = query_all.astype(jnp.float32) + first.astype(jnp.float32)
    heads = stream.reshape(SECTIONS, SLICE, QUERY_HEADS, HEAD_SIZE)
    norm = jnp.sqrt(lax.optimization_barrier(jnp.mean(heads * heads, axis=-1, keepdims=True)) + 1e-06)
    next_queries = ((heads / norm).reshape(SECTIONS, SLICE, QW) * gain).astype(jnp.bfloat16)
    moved_q = jnp.roll(next_queries, 1, axis=0)
    moved_k = jnp.roll(key_all, 1, axis=0)
    moved_v = jnp.roll(value_all, 1, axis=0)
    second = attend(moved_q, moved_k, moved_v, cache_k, cache_v, lent_keys, lent_values, lent_len, slice_index, lend_block[1], sinks).astype(jnp.bfloat16)
    return (first.reshape(SECTIONS * SLICE, QW), second.reshape(SECTIONS * SLICE, QW))
```

```python
import functools

import jax
import jax.numpy as jnp
from jax import lax
from jax.experimental import pallas as pl
from jax.experimental.pallas import tpu as pltpu
from jax.sharding import PartitionSpec as P

QUERY_HEADS = 64
KEY_VALUE_HEADS = 8
HEAD_SIZE = 64
QB = 64
REACH = 3
GROUP = QUERY_HEADS // KEY_VALUE_HEADS
LANES = 128
PAIR_KEYS = 2 * HEAD_SIZE
PAIR_QUERIES = 2 * GROUP * HEAD_SIZE
STEPS_OF_HEADS = KEY_VALUE_HEADS // 2
NEG = -1e30
KEY_CHUNK = 256
QW = QUERY_HEADS * HEAD_SIZE


def from_behind(block, axis, distance):
    devices = range(lax.axis_size(axis))
    route = [((i - distance) % len(devices), i) for i in devices]
    return lax.ppermute(block, axis, route)


def half_lanes(rows):
    return lax.broadcasted_iota(jnp.int32, (rows, LANES), 1) < HEAD_SIZE


def both_sides(block, head):
    low = half_lanes(block.shape[0])
    turned = jnp.concatenate([block[:, HEAD_SIZE:], block[:, :HEAD_SIZE]], axis=1)
    zero = jnp.zeros_like(block)
    at_low, at_high = (block, turned) if head == 0 else (turned, block)
    return jnp.where(low, at_low, zero), jnp.where(low, zero, at_high)


def attend_pair(queries, keys, values, head, mask):
    count = keys.shape[0]
    low_keys, high_keys = both_sides(keys, head)
    key_matrix = jnp.concatenate([low_keys, high_keys], axis=0)
    score = lax.dot_general(
        queries, key_matrix, (((1,), (1,)), ((), ())), preferred_element_type=jnp.float32
    )
    weights = []
    peaks = []
    for side in range(2):
        part = mask(score[:, side * count : (side + 1) * count])
        peak = jnp.max(part, axis=1, keepdims=True)
        weights.append(jnp.exp(part - peak).astype(jnp.bfloat16))
        peaks.append(peak)
    low_values, high_values = both_sides(values, head)
    low = half_lanes(count)
    one = jnp.ones((count, LANES), jnp.bfloat16)
    zero = jnp.zeros((count, LANES), jnp.bfloat16)
    value_matrix = jnp.concatenate(
        [
            jnp.concatenate([low_values, jnp.where(low, one, zero)], axis=1),
            jnp.concatenate([high_values, jnp.where(low, zero, one)], axis=1),
        ],
        axis=0,
    )
    summed = jnp.dot(
        jnp.concatenate(weights, axis=1), value_matrix, preferred_element_type=jnp.float32
    )
    total = summed[:, LANES:]
    out = summed[:, :LANES] / total
    lse = jnp.where(half_lanes(queries.shape[0]), peaks[0], peaks[1]) + jnp.log(total)
    return out, lse


def stacked(query_ref, head):
    base = head * GROUP * HEAD_SIZE
    pairs = [
        query_ref[:, base + p * LANES : base + (p + 1) * LANES] for p in range(GROUP // 2)
    ]
    return jnp.concatenate(pairs, axis=0) * jnp.bfloat16(HEAD_SIZE ** (-0.5))


def note_lse(stat, lse, rows, step, head):
    lane = lax.broadcasted_iota(jnp.int32, (rows, LANES), 1) % HEAD_SIZE
    for p in range(GROUP // 2):
        piece = lse[p * rows : (p + 1) * rows]
        for side in range(2):
            number = step * 2 * GROUP + head * GROUP + 2 * p + side
            column = piece[:, side * HEAD_SIZE : side * HEAD_SIZE + 1]
            stat = jnp.where(lane == number, column, stat)
    return stat


def lent_kernel(slot, len_ref, query_ref, key_ref, value_ref, out_ref, stat_ref):
    step = pl.program_id(0)
    rows = query_ref.shape[0]
    lent_rows = key_ref.shape[2]
    length = len_ref[0, slot]
    chunk = KEY_CHUNK if lent_rows % KEY_CHUNK == 0 else lent_rows

    @pl.when(step == 0)
    def _():
        stat_ref[...] = jnp.zeros_like(stat_ref)

    for n in range(1, lent_rows // chunk + 1):
        count = n * chunk

        @pl.when((length > count - chunk) & (length <= count))
        def _(count=count):
            def mask(part):
                tail = part[:, count - chunk :]
                at = lax.broadcasted_iota(jnp.int32, tail.shape, 1) + (count - chunk)
                tail = jnp.where(at < length, tail, NEG)
                if count == chunk:
                    return tail
                return jnp.concatenate([part[:, : count - chunk], tail], axis=1)

            stat = stat_ref[...]
            for head in range(2):
                out, lse = attend_pair(
                    stacked(query_ref, head),
                    key_ref[0, 0, :count, :],
                    value_ref[0, 0, :count, :],
                    head,
                    mask,
                )
                stat = note_lse(stat, lse, rows, step, head)
                for p in range(GROUP // 2):
                    start = pl.multiple_of(
                        step * PAIR_QUERIES + head * GROUP * HEAD_SIZE + p * LANES, LANES
                    )
                    out_ref[:, pl.ds(start, LANES)] = out[p * rows : (p + 1) * rows].astype(
                        jnp.bfloat16
                    )
            stat_ref[...] = stat

    @pl.when(step == pl.num_programs(0) - 1)
    def _():
        stat = stat_ref[...]
        high = stat.astype(jnp.bfloat16)
        rest = (stat - high.astype(jnp.float32)).astype(jnp.bfloat16)
        out_ref[:, QW:] = jnp.where(half_lanes(rows), high, rest)


def lent_terms(slot, queries, lent_keys, lent_values, lent_len):
    rows = queries.shape[0]
    lent_rows = lent_keys.shape[2]
    lent_spec = pl.BlockSpec((1, 1, lent_rows, PAIR_KEYS), lambda i, n: (0, slot, 0, i))
    return pl.pallas_call(
        functools.partial(lent_kernel, slot),
        out_shape=jax.ShapeDtypeStruct((rows, QW + LANES), jnp.bfloat16),
        grid_spec=pltpu.PrefetchScalarGridSpec(
            num_scalar_prefetch=1,
            grid=(STEPS_OF_HEADS,),
            in_specs=[
                pl.BlockSpec((rows, PAIR_QUERIES), lambda i, n: (0, i)),
                lent_spec,
                lent_spec,
            ],
            out_specs=pl.BlockSpec((rows, QW + LANES), lambda i, n: (0, 0)),
            scratch_shapes=[pltpu.VMEM((rows, LANES), jnp.float32)],
        ),
        cost_estimate=pl.CostEstimate(
            flops=16 * rows * lent_rows * QW,
            bytes_accessed=4 * lent_rows * KEY_VALUE_HEADS * HEAD_SIZE,
            transcendentals=rows * QUERY_HEADS * lent_rows,
        ),
        name=f"lent_{slot}",
    )(lent_len, queries, lent_keys, lent_values)


def local_kernel(
    index_ref, query_ref, cache_key_ref, cache_value_ref, key_ref, value_ref, out_ref, stat_ref
):
    step = pl.program_id(0)
    rows = query_ref.shape[0]
    cache_rows = cache_key_ref.shape[0]
    own_rows = index_ref[0] * rows

    def mask(part):
        row = lax.broadcasted_iota(jnp.int32, part.shape, 0) % rows
        at = lax.broadcasted_iota(jnp.int32, part.shape, 1)
        valid = (at < own_rows) | ((at >= cache_rows) & (at - cache_rows <= row))
        return jnp.where(valid, part, NEG)

    @pl.when(step == 0)
    def _():
        stat_ref[...] = jnp.zeros_like(stat_ref)

    keys = jnp.concatenate([cache_key_ref[...], key_ref[...]], axis=0)
    values = jnp.concatenate([cache_value_ref[...], value_ref[...]], axis=0)
    stat = stat_ref[...]
    for head in range(2):
        out, lse = attend_pair(stacked(query_ref, head), keys, values, head, mask)
        stat = note_lse(stat, lse, rows, step, head)
        for p in range(GROUP // 2):
            start = head * GROUP * HEAD_SIZE + p * LANES
            out_ref[:, start : start + LANES] = out[p * rows : (p + 1) * rows]
    stat_ref[...] = stat


def local_terms(queries, cache_keys, cache_values, own_keys, own_values, slice_index):
    rows = queries.shape[0]
    cache_rows = cache_keys.shape[0]
    cache_spec = pl.BlockSpec((cache_rows, PAIR_KEYS), lambda i, n: (0, i))
    own_spec = pl.BlockSpec((rows, PAIR_KEYS), lambda i, n: (0, i))
    return pl.pallas_call(
        local_kernel,
        out_shape=(
            jax.ShapeDtypeStruct((rows, QW), jnp.float32),
            jax.ShapeDtypeStruct((rows, LANES), jnp.float32),
        ),
        grid_spec=pltpu.PrefetchScalarGridSpec(
            num_scalar_prefetch=1,
            grid=(STEPS_OF_HEADS,),
            in_specs=[
                pl.BlockSpec((rows, PAIR_QUERIES), lambda i, n: (0, i)),
                cache_spec,
                cache_spec,
                own_spec,
                own_spec,
            ],
            out_specs=(
                pl.BlockSpec((rows, PAIR_QUERIES), lambda i, n: (0, i)),
                pl.BlockSpec((rows, LANES), lambda i, n: (0, 0)),
            ),
        ),
        cost_estimate=pl.CostEstimate(
            flops=16 * rows * (cache_rows + rows) * QW,
            bytes_accessed=4 * (cache_rows + rows) * KEY_VALUE_HEADS * HEAD_SIZE,
            transcendentals=rows * QUERY_HEADS * (cache_rows + rows),
        ),
        name="local",
    )(slice_index, queries, cache_keys, cache_values, own_keys, own_values)


def spread_dot(left, right):
    high = left.astype(jnp.bfloat16)
    rest = (left - high.astype(jnp.float32)).astype(jnp.bfloat16)
    return jnp.dot(high, right, preferred_element_type=jnp.float32) + jnp.dot(
        rest, right, preferred_element_type=jnp.float32
    )


def combine_kernel(with_next, *refs):
    plan_ref, next_plan_ref, local_ref, local_stat_ref, sink_ref = refs[:5]
    outs = refs[5 : 5 + REACH]
    stats = refs[5 + REACH : 5 + 2 * REACH]
    rest = refs[5 + 2 * REACH :]
    step = pl.program_id(0)
    rows, width = local_ref.shape
    halves = rows // QB
    sink = jnp.broadcast_to(sink_ref[...], (rows, LANES))
    lses = [local_stat_ref[...]]
    for d in range(REACH):
        stat = stats[d][...].astype(jnp.float32)
        lse = stat + pltpu.roll(stat, HEAD_SIZE, 1)
        lses.append(
            jnp.concatenate(
                [jnp.where(plan_ref[d] == half, lse, NEG) for half in range(halves)], axis=0
            )
        )
    top = functools.reduce(jnp.maximum, lses, sink)
    factors = [jnp.exp(lse - top) for lse in lses]
    denom = functools.reduce(lambda a, b: a + b, factors) + jnp.exp(sink - top)
    head_of_row = lax.broadcasted_iota(jnp.int32, (LANES, width), 0) % HEAD_SIZE
    head_of_lane = lax.broadcasted_iota(jnp.int32, (LANES, width), 1) // HEAD_SIZE
    expand = (head_of_row == head_of_lane + step * (width // HEAD_SIZE)).astype(jnp.bfloat16)
    low = half_lanes(rows)
    spread = []
    for factor in factors:
        share = factor / denom
        high = share.astype(jnp.bfloat16)
        split = jnp.where(low, high, (share - high.astype(jnp.float32)).astype(jnp.bfloat16))
        spread.append(jnp.dot(split, expand, preferred_element_type=jnp.float32))
    result = local_ref[...] * spread[0]
    for d in range(REACH):
        block = outs[d][...].astype(jnp.float32)
        result = result + jnp.concatenate([block] * halves, axis=0) * spread[d + 1]
    rounded = result.astype(jnp.bfloat16)
    if not with_next:
        rest[0][...] = rounded
        return
    query_ref, gain_ref, first_ref, next_ref = rest[:4]
    blocks = rest[4:]
    first_ref[...] = rounded
    stream = query_ref[...].astype(jnp.float32) + rounded.astype(jnp.float32)
    ones = (
        lax.broadcasted_iota(jnp.int32, (LANES, LANES), 0) // HEAD_SIZE
        == lax.broadcasted_iota(jnp.int32, (LANES, LANES), 1) // HEAD_SIZE
    ).astype(jnp.bfloat16)
    square = stream * stream
    sums = jnp.concatenate(
        [
            spread_dot(square[:, c : c + LANES], ones)
            for c in range(0, width, LANES)
        ],
        axis=1,
    )
    norm = jnp.sqrt(sums * (1.0 / HEAD_SIZE) + 1e-06)
    following = ((stream / norm) * gain_ref[...]).astype(jnp.bfloat16)
    next_ref[...] = following
    for d in range(REACH):
        block = following[:QB]
        for half in range(1, halves):
            block = jnp.where(
                next_plan_ref[d] == half, following[half * QB : (half + 1) * QB], block
            )
        blocks[d][...] = block


def combine(plan, next_plan, local, returned, sinks, queries=None, gain=None):
    local_out, local_stat = local
    rows = local_out.shape[0]
    width = PAIR_QUERIES
    with_next = queries is not None
    wide = pl.BlockSpec((rows, width), lambda i, a, b: (0, i))
    block = pl.BlockSpec((QB, width), lambda i, a, b: (0, i))
    in_specs = [
        wide,
        pl.BlockSpec((rows, LANES), lambda i, a, b: (0, 0)),
        pl.BlockSpec((1, LANES), lambda i, a, b: (0, 0)),
    ]
    in_specs += [block] * REACH
    in_specs += [pl.BlockSpec((QB, LANES), lambda i, a, b: (0, QW // LANES))] * REACH
    args = [local_out, local_stat, sinks, *returned, *returned]
    shape = jax.ShapeDtypeStruct((rows, QW), jnp.bfloat16)
    if with_next:
        in_specs += [wide, pl.BlockSpec((1, width), lambda i, a, b: (0, i))]
        args += [queries, gain]
        out_shape = (shape, shape) + (jax.ShapeDtypeStruct((QB, QW), jnp.bfloat16),) * REACH
        out_specs = (wide, wide) + (block,) * REACH
    else:
        out_shape = shape
        out_specs = wide
    return pl.pallas_call(
        functools.partial(combine_kernel, with_next),
        out_shape=out_shape,
        grid_spec=pltpu.PrefetchScalarGridSpec(
            num_scalar_prefetch=2,
            grid=(QW // width,),
            in_specs=in_specs,
            out_specs=out_specs,
        ),
        name="combine",
    )(plan, next_plan, *args)


def body(
    queries,
    slice_keys,
    slice_values,
    cache_keys,
    cache_values,
    lent_keys,
    lent_values,
    lent_len,
    slice_index,
    lend_block,
    sinks,
    gain,
):
    sink_row = jnp.concatenate([sinks, sinks])[None, :]
    gain_row = gain[None, :]
    first_plan = lend_block[0, 0]
    second_plan = lend_block[1, 0]
    blocks = [
        lax.dynamic_slice_in_dim(queries, first_plan[d] * QB, QB, 0) for d in range(REACH)
    ]
    arrived = [from_behind(blocks[d], "section", d + 1) for d in range(REACH)]
    next_plan = from_behind(second_plan, "section", -1)
    moved_k = from_behind(slice_keys, "section", 1)
    moved_v = from_behind(slice_values, "section", 1)

    def returns(arrived):
        terms = []
        for d in range(REACH):
            term = lent_terms(d, arrived[d], lent_keys, lent_values, lent_len)
            terms.append(from_behind(term, "section", -(d + 1)))
        return terms

    local = local_terms(queries, cache_keys, cache_values, slice_keys, slice_values, slice_index)
    first, following, *blocks = combine(
        first_plan, next_plan, local, returns(arrived), sink_row, queries, gain_row
    )
    arrived = [from_behind(blocks[d], "section", d + 2) for d in range(REACH)]
    moved_q = from_behind(following, "section", 1)
    returned = returns(arrived)
    local = local_terms(moved_q, cache_keys, cache_values, moved_k, moved_v, slice_index)
    second = combine(second_plan, second_plan, local, returned, sink_row)
    return (first, second)


def solution(mesh):
    placed = (
        P(("groups", "section"), None),
        P(("groups", "section"), None),
        P(("groups", "section"), None),
        P(("groups", "section"), None),
        P(("groups", "section"), None),
        P(("groups", "section"), None, None, None),
        P(("groups", "section"), None, None, None),
        P(("groups", "section"), None),
        P(("groups", "section")),
        P(None, ("groups", "section"), None),
        P(),
        P(),
    )
    return jax.shard_map(
        body,
        mesh=mesh,
        in_specs=placed,
        out_specs=(P(("groups", "section"), None), P(("groups", "section"), None)),
        check_vma=False,
    )
```

```python
import functools

import jax
import jax.numpy as jnp
from jax import lax
from jax.experimental import pallas as pl
from jax.experimental.pallas import tpu as pltpu
from jax.sharding import PartitionSpec as P

QUERY_HEADS = 64
KEY_VALUE_HEADS = 8
HEAD_SIZE = 64
QB = 64
REACH = 3
GROUP = QUERY_HEADS // KEY_VALUE_HEADS
LANES = 128
PAIR_KEYS = 2 * HEAD_SIZE
PAIR_QUERIES = 2 * GROUP * HEAD_SIZE
STEPS_OF_HEADS = KEY_VALUE_HEADS // 2
NEG = -1e30
KEY_CHUNK = 256
QW = QUERY_HEADS * HEAD_SIZE
CHUNKS = 2
CHUNK_HEADS = QUERY_HEADS // CHUNKS
CW = QW // CHUNKS
CHUNK_PAIRS = STEPS_OF_HEADS // CHUNKS
PARTS = 3


def from_behind(block, axis, distance):
    devices = range(lax.axis_size(axis))
    route = [((i - distance) % len(devices), i) for i in devices]
    return lax.ppermute(block, axis, route)


def half_lanes(rows):
    return lax.broadcasted_iota(jnp.int32, (rows, LANES), 1) < HEAD_SIZE


def scores_of(query_ref, keys, head):
    base = head * GROUP * HEAD_SIZE
    pairs = [
        query_ref[:, base + p * LANES : base + (p + 1) * LANES] for p in range(GROUP // 2)
    ]
    straight = jnp.concatenate(pairs, axis=0) * jnp.bfloat16(HEAD_SIZE ** (-0.5))
    turned = jnp.concatenate([straight[:, HEAD_SIZE:], straight[:, :HEAD_SIZE]], axis=1)
    low = half_lanes(keys.shape[0])
    zero = jnp.zeros_like(keys)
    if head == 0:
        key_matrix = jnp.where(low, keys, zero)
        rows = jnp.concatenate([straight, turned], axis=0)
    else:
        key_matrix = jnp.where(low, zero, keys)
        rows = jnp.concatenate([turned, straight], axis=0)
    return lax.dot_general(
        rows, key_matrix, (((1,), (1,)), ((), ())), preferred_element_type=jnp.float32
    )


def attend_scores(score, values, head, mask):
    score = mask(score)
    peak = jnp.max(score, axis=1, keepdims=True)
    weight = jnp.exp(score - peak).astype(jnp.bfloat16)
    turned = jnp.concatenate([values[:, HEAD_SIZE:], values[:, :HEAD_SIZE]], axis=1)
    at_low, at_high = (values, turned) if head == 0 else (turned, values)
    low = half_lanes(values.shape[0])
    one = jnp.ones_like(values)
    value_matrix = jnp.concatenate(
        [jnp.where(low, at_low, one), jnp.where(low, one, at_high)], axis=1
    )
    summed = jnp.dot(weight, value_matrix, preferred_element_type=jnp.float32)
    n = score.shape[0] // 2
    low = half_lanes(n)
    even, odd = summed[:n], summed[n:]
    total = jnp.where(low, even[:, LANES:], odd[:, :LANES])
    out = jnp.where(low, even[:, :LANES], odd[:, LANES:]) / total
    return out, jnp.where(low, peak[:n], peak[n:]) + jnp.log(total)


def attend(query_ref, keys, values, mask):
    scores = [scores_of(query_ref, keys, head) for head in range(2)]
    return [attend_scores(scores[head], values, head, mask) for head in range(2)]


def note_lse(stat, lse, rows, step, head):
    lane = lax.broadcasted_iota(jnp.int32, (rows, LANES), 1) % CHUNK_HEADS
    for p in range(GROUP // 2):
        piece = lse[p * rows : (p + 1) * rows]
        for side in range(2):
            number = step * 2 * GROUP + head * GROUP + 2 * p + side
            column = piece[:, side * HEAD_SIZE : side * HEAD_SIZE + 1]
            stat = jnp.where(lane == number, column, stat)
    return stat


def split_parts(value):
    group = lax.broadcasted_iota(jnp.int32, value.shape, 1) // CHUNK_HEADS
    parts = jnp.zeros(value.shape, jnp.bfloat16)
    rest = value
    for part in range(PARTS):
        rounded = rest.astype(jnp.bfloat16)
        parts = jnp.where(group == part, rounded, parts)
        rest = rest - rounded.astype(jnp.float32)
    return parts


def lent_kernel(orders, len_ref, *refs):
    queries = refs[:REACH]
    key_ref, value_ref = refs[REACH : REACH + 2]
    outs = refs[REACH + 2 + orders : 2 * REACH + 2 + orders]
    query_ref, out_ref, stat_ref = refs[2 * REACH + 2 + orders :]
    slot, step = pl.program_id(0), pl.program_id(1)
    rows = query_ref.shape[0]
    lent_rows = key_ref.shape[2]
    length = len_ref[0, slot]
    chunk = KEY_CHUNK if lent_rows % KEY_CHUNK == 0 else lent_rows

    for d in range(REACH):

        @pl.when(slot == d)
        def _(d=d):
            query_ref[...] = queries[d][...]

    @pl.when(step == 0)
    def _():
        stat_ref[...] = jnp.zeros_like(stat_ref)

    for n in range(1, lent_rows // chunk + 1):
        count = n * chunk

        @pl.when((length > count - chunk) & (length <= count))
        def _(count=count):
            def mask(part):
                tail = part[:, count - chunk :]
                at = lax.broadcasted_iota(jnp.int32, tail.shape, 1) + (count - chunk)
                tail = jnp.where(at < length, tail, NEG)
                if count == chunk:
                    return tail
                return jnp.concatenate([part[:, : count - chunk], tail], axis=1)

            stat = stat_ref[...]
            both = attend(query_ref, key_ref[0, 0, :count, :], value_ref[0, 0, :count, :], mask)
            for head in range(2):
                out, lse = both[head]
                stat = note_lse(stat, lse, rows, step, head)
                for p in range(GROUP // 2):
                    start = head * GROUP * HEAD_SIZE + p * LANES
                    out_ref[:, start : start + LANES] = out[p * rows : (p + 1) * rows].astype(
                        jnp.bfloat16
                    )
            stat_ref[...] = stat

    for d in range(REACH):

        @pl.when(slot == d)
        def _(d=d):
            start = pl.multiple_of(step * PAIR_QUERIES, PAIR_QUERIES)
            outs[d][:, pl.ds(start, PAIR_QUERIES)] = out_ref[...]
            outs[d][:, CW:] = split_parts(stat_ref[...])


def lent_terms(part, queries, lent_keys, lent_values, lent_len, order):
    rows = queries[0].shape[0]
    lent_rows = lent_keys.shape[2]
    base = part * CHUNK_PAIRS
    lent_spec = pl.BlockSpec((1, 1, lent_rows, PAIR_KEYS), lambda d, i, n: (0, d, 0, base + i))
    return pl.pallas_call(
        functools.partial(lent_kernel, len(order)),
        out_shape=(jax.ShapeDtypeStruct((rows, CW + LANES), jnp.bfloat16),) * REACH,
        grid_spec=pltpu.PrefetchScalarGridSpec(
            num_scalar_prefetch=1,
            grid=(REACH, CHUNK_PAIRS),
            in_specs=[pl.BlockSpec((rows, PAIR_QUERIES), lambda d, i, n: (0, i))] * REACH
            + [lent_spec, lent_spec]
            + [pl.BlockSpec(memory_space=pl.ANY)] * len(order),
            out_specs=(pl.BlockSpec((rows, CW + LANES), lambda d, i, n: (0, 0)),) * REACH,
            scratch_shapes=[
                pltpu.VMEM((rows, PAIR_QUERIES), jnp.bfloat16),
                pltpu.VMEM((rows, PAIR_QUERIES), jnp.bfloat16),
                pltpu.VMEM((rows, LANES), jnp.float32),
            ],
        ),
        cost_estimate=pl.CostEstimate(
            flops=16 * REACH * rows * lent_rows * CW,
            bytes_accessed=4 * REACH * lent_rows * CHUNK_PAIRS * PAIR_KEYS,
            transcendentals=REACH * rows * CHUNK_HEADS * lent_rows,
        ),
        name="lent",
    )(lent_len, *queries, lent_keys, lent_values, *order)


def local_kernel(
    orders, index_ref, query_ref, cache_key_ref, cache_value_ref, key_ref, value_ref, *refs
):
    out_ref, stat_ref = refs[orders:]
    step = pl.program_id(0)
    rows = query_ref.shape[0]
    cache_rows = cache_key_ref.shape[0]
    own_rows = index_ref[0] * rows

    def mask(part):
        row = lax.broadcasted_iota(jnp.int32, part.shape, 0) % rows
        at = lax.broadcasted_iota(jnp.int32, part.shape, 1)
        valid = (at < own_rows) | ((at >= cache_rows) & (at - cache_rows <= row))
        return jnp.where(valid, part, NEG)

    @pl.when(step == 0)
    def _():
        stat_ref[...] = jnp.zeros_like(stat_ref)

    keys = jnp.concatenate([cache_key_ref[...], key_ref[...]], axis=0)
    values = jnp.concatenate([cache_value_ref[...], value_ref[...]], axis=0)
    stat = stat_ref[...]
    both = attend(query_ref, keys, values, mask)
    for head in range(2):
        out, lse = both[head]
        stat = note_lse(stat, lse, rows, step, head)
        for p in range(GROUP // 2):
            start = head * GROUP * HEAD_SIZE + p * LANES
            out_ref[:, start : start + LANES] = out[p * rows : (p + 1) * rows].astype(
                jnp.bfloat16
            )
    stat_ref[...] = stat


def local_terms(
    part, queries, cache_keys, cache_values, own_keys, own_values, slice_index, order
):
    rows = queries.shape[0]
    cache_rows = cache_keys.shape[0]
    base = part * CHUNK_PAIRS
    query_base = base if queries.shape[1] == QW else 0
    cache_spec = pl.BlockSpec((cache_rows, PAIR_KEYS), lambda i, n: (0, base + i))
    own_spec = pl.BlockSpec((rows, PAIR_KEYS), lambda i, n: (0, base + i))
    return pl.pallas_call(
        functools.partial(local_kernel, len(order)),
        out_shape=(
            jax.ShapeDtypeStruct((rows, CW), jnp.bfloat16),
            jax.ShapeDtypeStruct((rows, LANES), jnp.float32),
        ),
        grid_spec=pltpu.PrefetchScalarGridSpec(
            num_scalar_prefetch=1,
            grid=(CHUNK_PAIRS,),
            in_specs=[
                pl.BlockSpec((rows, PAIR_QUERIES), lambda i, n: (0, query_base + i)),
                cache_spec,
                cache_spec,
                own_spec,
                own_spec,
            ]
            + [pl.BlockSpec(memory_space=pl.ANY)] * len(order),
            out_specs=(
                pl.BlockSpec((rows, PAIR_QUERIES), lambda i, n: (0, i)),
                pl.BlockSpec((rows, LANES), lambda i, n: (0, 0)),
            ),
        ),
        cost_estimate=pl.CostEstimate(
            flops=16 * rows * (cache_rows + rows) * CW,
            bytes_accessed=4 * (cache_rows + rows) * CHUNK_PAIRS * PAIR_KEYS,
            transcendentals=rows * CHUNK_HEADS * (cache_rows + rows),
        ),
        name="local",
    )(slice_index, queries, cache_keys, cache_values, own_keys, own_values, *order)


def spread_dot(left, right):
    high = left.astype(jnp.bfloat16)
    rest = (left - high.astype(jnp.float32)).astype(jnp.bfloat16)
    return jnp.dot(high, right, preferred_element_type=jnp.float32) + jnp.dot(
        rest, right, preferred_element_type=jnp.float32
    )


def combine_kernel(with_next, extra, *refs):
    plan_ref, next_plan_ref, local_ref, local_stat_ref, sink_ref = refs[:5]
    outs = refs[5 : 5 + REACH]
    stats = refs[5 + REACH : 5 + 2 * REACH]
    rest = refs[5 + 2 * REACH :]
    inputs = 2 if with_next else 0
    rest = rest[:inputs] + rest[inputs + extra :]
    step = pl.program_id(0)
    rows, width = local_ref.shape
    halves = rows // QB
    sink = jnp.broadcast_to(sink_ref[...], (rows, LANES))
    lses = [local_stat_ref[...]]
    for d in range(REACH):
        stat = stats[d][...].astype(jnp.float32)
        lse = stat
        for part in range(1, LANES // CHUNK_HEADS):
            lse = lse + pltpu.roll(stat, part * CHUNK_HEADS, 1)
        lses.append(
            jnp.concatenate(
                [jnp.where(plan_ref[d] == half, lse, NEG) for half in range(halves)], axis=0
            )
        )
    top = functools.reduce(jnp.maximum, lses, sink)
    factors = [jnp.exp(lse - top) for lse in lses]
    denom = functools.reduce(lambda a, b: a + b, factors) + jnp.exp(sink - top)
    head_of_row = lax.broadcasted_iota(jnp.int32, (LANES, width), 0) % CHUNK_HEADS
    head_of_lane = lax.broadcasted_iota(jnp.int32, (LANES, width), 1) // HEAD_SIZE
    expand = (head_of_row == head_of_lane + step * (width // HEAD_SIZE)).astype(jnp.bfloat16)
    spread = []
    for factor in factors:
        share = factor / denom
        spread.append(jnp.dot(split_parts(share), expand, preferred_element_type=jnp.float32))
    result = local_ref[...].astype(jnp.float32) * spread[0]
    for d in range(REACH):
        block = outs[d][...].astype(jnp.float32)
        result = result + jnp.concatenate([block] * halves, axis=0) * spread[d + 1]
    rounded = result.astype(jnp.bfloat16)
    if not with_next:
        rest[0][...] = rounded
        return
    query_ref, gain_ref, first_ref, next_ref = rest[:4]
    blocks = rest[4:]
    first_ref[...] = rounded
    stream = query_ref[...].astype(jnp.float32) + rounded.astype(jnp.float32)
    ones = (
        lax.broadcasted_iota(jnp.int32, (LANES, LANES), 0) // HEAD_SIZE
        == lax.broadcasted_iota(jnp.int32, (LANES, LANES), 1) // HEAD_SIZE
    ).astype(jnp.bfloat16)
    square = stream * stream
    sums = jnp.concatenate(
        [
            spread_dot(square[:, c : c + LANES], ones)
            for c in range(0, width, LANES)
        ],
        axis=1,
    )
    scale = lax.rsqrt(sums * (1.0 / HEAD_SIZE) + 1e-06)
    following = ((stream * scale) * gain_ref[...]).astype(jnp.bfloat16)
    next_ref[...] = following
    for d in range(REACH):
        block = following[:QB]
        for half in range(1, halves):
            block = jnp.where(
                next_plan_ref[d] == half, following[half * QB : (half + 1) * QB], block
            )
        blocks[d][...] = block


def combine(part, plan, next_plan, local, returned, sinks, earlier, order, queries=None, gain=None):
    local_out, local_stat = local
    rows = local_out.shape[0]
    width = PAIR_QUERIES
    base = part * CHUNK_PAIRS
    with_next = queries is not None
    here = pl.BlockSpec((rows, width), lambda i, a, b: (0, i))
    wide = pl.BlockSpec((rows, width), lambda i, a, b: (0, base + i))
    block = pl.BlockSpec((QB, width), lambda i, a, b: (0, i))
    in_specs = [
        here,
        pl.BlockSpec((rows, LANES), lambda i, a, b: (0, 0)),
        pl.BlockSpec((1, LANES), lambda i, a, b: (0, part)),
    ]
    in_specs += [block] * REACH
    in_specs += [pl.BlockSpec((QB, LANES), lambda i, a, b: (0, CW // LANES))] * REACH
    args = [local_out, local_stat, sinks, *returned, *returned]
    shape = jax.ShapeDtypeStruct((rows, QW), jnp.bfloat16)
    if with_next:
        in_specs += [wide, pl.BlockSpec((1, width), lambda i, a, b: (0, base + i))]
        args += [queries, gain]
        out_shape = (shape, jax.ShapeDtypeStruct((rows, CW), jnp.bfloat16))
        out_shape += (jax.ShapeDtypeStruct((QB, CW), jnp.bfloat16),) * REACH
        out_specs = (wide, here) + (block,) * REACH
    else:
        out_shape = (shape,)
        out_specs = (wide,)
    extra = list(order)
    aliases = {}
    if earlier is not None:
        extra.append(earlier)
        aliases = {2 + len(args) + len(extra) - 1: 0}
    in_specs += [pl.BlockSpec(memory_space=pl.ANY)] * len(extra)
    return pl.pallas_call(
        functools.partial(combine_kernel, with_next, len(extra)),
        out_shape=out_shape,
        grid_spec=pltpu.PrefetchScalarGridSpec(
            num_scalar_prefetch=2,
            grid=(CW // width,),
            in_specs=in_specs,
            out_specs=out_specs,
        ),
        input_output_aliases=aliases,
        name="combine",
    )(plan, next_plan, *args, *extra)


def body(
    queries,
    slice_keys,
    slice_values,
    cache_keys,
    cache_values,
    lent_keys,
    lent_values,
    lent_len,
    slice_index,
    lend_block,
    sinks,
    gain,
):
    sink_row = jnp.tile(sinks.reshape(CHUNKS, 1, CHUNK_HEADS), (1, LANES // CHUNK_HEADS, 1))
    sink_row = sink_row.reshape(1, CHUNKS * LANES)
    gain_row = gain[None, :]
    first_plan = lend_block[0, 0]
    second_plan = lend_block[1, 0]

    def block_of(part, d):
        rows = lax.dynamic_slice_in_dim(queries, first_plan[d] * QB, QB, 0)
        return rows[:, part * CW : (part + 1) * CW]

    def send(blocks, extra):
        return [from_behind(blocks[d], "section", d + 1 + extra) for d in range(REACH)]

    def lent(part, arrived, order):
        return lent_terms(part, arrived, lent_keys, lent_values, lent_len, order)

    def back(terms):
        return [from_behind(terms[d], "section", -(d + 1)) for d in range(REACH)]

    def local(part, current, own_keys, own_values, order):
        return local_terms(
            part, current, cache_keys, cache_values, own_keys, own_values, slice_index, order
        )

    arrived = [send([block_of(part, d) for d in range(REACH)], 0) for part in range(CHUNKS)]
    next_plan = from_behind(second_plan, "section", -1)
    moved_k = from_behind(slice_keys, "section", 1)
    moved_v = from_behind(slice_values, "section", 1)

    local_0 = local(0, queries, slice_keys, slice_values, [])
    terms_0 = lent(0, arrived[0], [local_0[1]])
    back_0 = back(terms_0)
    terms_1 = lent(1, arrived[1], [terms_0[0]])
    back_1 = back(terms_1)
    first, follow_0, *blocks_0 = combine(
        0, first_plan, next_plan, local_0, back_0, sink_row, None, [terms_1[0]], queries, gain_row
    )
    next_0 = send(blocks_0, 1)
    moved_0 = from_behind(follow_0, "section", 1)
    local_1 = local(1, queries, slice_keys, slice_values, [follow_0, moved_k, moved_v])
    first, follow_1, *blocks_1 = combine(
        1, first_plan, next_plan, local_1, back_1, sink_row, first, [], queries, gain_row
    )
    next_1 = send(blocks_1, 1)
    moved_1 = from_behind(follow_1, "section", 1)
    terms_0 = lent(0, next_0, [follow_1])
    back_0 = back(terms_0)
    local_0 = local(0, moved_0, moved_k, moved_v, [terms_0[0]])
    terms_1 = lent(1, next_1, [local_0[1]])
    back_1 = back(terms_1)
    (second,) = combine(
        0, second_plan, second_plan, local_0, back_0, sink_row, None, [terms_1[0]]
    )
    local_1 = local(1, moved_1, moved_k, moved_v, [terms_1[0], second])
    (second,) = combine(1, second_plan, second_plan, local_1, back_1, sink_row, second, [])
    return (first, second)


def solution(mesh):
    placed = (
        P(("groups", "section"), None),
        P(("groups", "section"), None),
        P(("groups", "section"), None),
        P(("groups", "section"), None),
        P(("groups", "section"), None),
        P(("groups", "section"), None, None, None),
        P(("groups", "section"), None, None, None),
        P(("groups", "section"), None),
        P(("groups", "section")),
        P(None, ("groups", "section"), None),
        P(),
        P(),
    )
    return jax.shard_map(
        body,
        mesh=mesh,
        in_specs=placed,
        out_specs=(P(("groups", "section"), None), P(("groups", "section"), None)),
        check_vma=False,
    )
```

```python
import functools

import jax
import jax.numpy as jnp
from jax import lax
from jax.experimental import pallas as pl
from jax.experimental.pallas import tpu as pltpu
from jax.sharding import PartitionSpec as P

QUERY_HEADS = 64
KEY_VALUE_HEADS = 8
HEAD_SIZE = 64
QB = 64
REACH = 3
GROUP = QUERY_HEADS // KEY_VALUE_HEADS
LANES = 128
PAIR_KEYS = 2 * HEAD_SIZE
PAIR_QUERIES = 2 * GROUP * HEAD_SIZE
STEPS_OF_HEADS = KEY_VALUE_HEADS // 2
NEG = -1e30
KEY_CHUNK = 256
QW = QUERY_HEADS * HEAD_SIZE
CHUNKS = 2
CHUNK_HEADS = QUERY_HEADS // CHUNKS
CW = QW // CHUNKS
CHUNK_PAIRS = STEPS_OF_HEADS // CHUNKS
PARTS = 3


def from_behind(block, axis, distance):
    devices = range(lax.axis_size(axis))
    route = [((i - distance) % len(devices), i) for i in devices]
    return lax.ppermute(block, axis, route)


def half_lanes(rows):
    return lax.broadcasted_iota(jnp.int32, (rows, LANES), 1) < HEAD_SIZE


def scores_of(query_ref, keys, head):
    base = head * GROUP * HEAD_SIZE
    pairs = [
        query_ref[:, base + p * LANES : base + (p + 1) * LANES] for p in range(GROUP // 2)
    ]
    straight = jnp.concatenate(pairs, axis=0) * jnp.bfloat16(HEAD_SIZE ** (-0.5))
    turned = jnp.concatenate([straight[:, HEAD_SIZE:], straight[:, :HEAD_SIZE]], axis=1)
    low = half_lanes(keys.shape[0])
    zero = jnp.zeros_like(keys)
    if head == 0:
        key_matrix = jnp.where(low, keys, zero)
        rows = jnp.concatenate([straight, turned], axis=0)
    else:
        key_matrix = jnp.where(low, zero, keys)
        rows = jnp.concatenate([turned, straight], axis=0)
    return lax.dot_general(
        rows, key_matrix, (((1,), (1,)), ((), ())), preferred_element_type=jnp.float32
    )


def attend_scores(score, values, head, mask):
    score = mask(score)
    peak = jnp.max(score, axis=1, keepdims=True)
    weight = jnp.exp(score - peak).astype(jnp.bfloat16)
    turned = jnp.concatenate([values[:, HEAD_SIZE:], values[:, :HEAD_SIZE]], axis=1)
    at_low, at_high = (values, turned) if head == 0 else (turned, values)
    low = half_lanes(values.shape[0])
    one = jnp.ones_like(values)
    value_matrix = jnp.concatenate(
        [jnp.where(low, at_low, one), jnp.where(low, one, at_high)], axis=1
    )
    summed = jnp.dot(weight, value_matrix, preferred_element_type=jnp.float32)
    n = score.shape[0] // 2
    low = half_lanes(n)
    even, odd = summed[:n], summed[n:]
    total = jnp.where(low, even[:, LANES:], odd[:, :LANES])
    out = jnp.where(low, even[:, :LANES], odd[:, LANES:]) / total
    return out, jnp.where(low, peak[:n], peak[n:]) + jnp.log(total)


def attend(query_ref, keys, values, mask):
    scores = [scores_of(query_ref, keys, head) for head in range(2)]
    return [attend_scores(scores[head], values, head, mask) for head in range(2)]


def note_lse(stat, lse, rows, step, head):
    lane = lax.broadcasted_iota(jnp.int32, (rows, LANES), 1) % CHUNK_HEADS
    for p in range(GROUP // 2):
        piece = lse[p * rows : (p + 1) * rows]
        for side in range(2):
            number = step * 2 * GROUP + head * GROUP + 2 * p + side
            column = piece[:, side * HEAD_SIZE : side * HEAD_SIZE + 1]
            stat = jnp.where(lane == number, column, stat)
    return stat


def split_parts(value):
    group = lax.broadcasted_iota(jnp.int32, value.shape, 1) // CHUNK_HEADS
    parts = jnp.zeros(value.shape, jnp.bfloat16)
    rest = value
    for part in range(PARTS):
        rounded = rest.astype(jnp.bfloat16)
        parts = jnp.where(group == part, rounded, parts)
        rest = rest - rounded.astype(jnp.float32)
    return parts


def lent_kernel(orders, len_ref, *refs):
    queries = refs[:REACH]
    key_ref, value_ref = refs[REACH : REACH + 2]
    outs = refs[REACH + 2 + orders : 2 * REACH + 2 + orders]
    query_ref, out_ref, stat_ref = refs[2 * REACH + 2 + orders :]
    slot, step = pl.program_id(0), pl.program_id(1)
    rows = query_ref.shape[0]
    lent_rows = key_ref.shape[2]
    length = len_ref[0, slot]
    chunk = KEY_CHUNK if lent_rows % KEY_CHUNK == 0 else lent_rows

    for d in range(REACH):

        @pl.when(slot == d)
        def _(d=d):
            query_ref[...] = queries[d][...]

    @pl.when(step == 0)
    def _():
        stat_ref[...] = jnp.zeros_like(stat_ref)

    for n in range(1, lent_rows // chunk + 1):
        count = n * chunk

        @pl.when((length > count - chunk) & (length <= count))
        def _(count=count):
            def mask(part):
                tail = part[:, count - chunk :]
                at = lax.broadcasted_iota(jnp.int32, tail.shape, 1) + (count - chunk)
                tail = jnp.where(at < length, tail, NEG)
                if count == chunk:
                    return tail
                return jnp.concatenate([part[:, : count - chunk], tail], axis=1)

            stat = stat_ref[...]
            both = attend(query_ref, key_ref[0, 0, :count, :], value_ref[0, 0, :count, :], mask)
            for head in range(2):
                out, lse = both[head]
                stat = note_lse(stat, lse, rows, step, head)
                for p in range(GROUP // 2):
                    start = head * GROUP * HEAD_SIZE + p * LANES
                    out_ref[:, start : start + LANES] = out[p * rows : (p + 1) * rows].astype(
                        jnp.bfloat16
                    )
            stat_ref[...] = stat

    for d in range(REACH):

        @pl.when(slot == d)
        def _(d=d):
            start = pl.multiple_of(step * PAIR_QUERIES, PAIR_QUERIES)
            outs[d][:, pl.ds(start, PAIR_QUERIES)] = out_ref[...]
            outs[d][:, CW:] = split_parts(stat_ref[...])


def lent_terms(part, queries, lent_keys, lent_values, lent_len, order):
    rows = queries[0].shape[0]
    lent_rows = lent_keys.shape[2]
    base = part * CHUNK_PAIRS
    lent_spec = pl.BlockSpec((1, 1, lent_rows, PAIR_KEYS), lambda d, i, n: (0, d, 0, base + i))
    return pl.pallas_call(
        functools.partial(lent_kernel, len(order)),
        out_shape=(jax.ShapeDtypeStruct((rows, CW + LANES), jnp.bfloat16),) * REACH,
        grid_spec=pltpu.PrefetchScalarGridSpec(
            num_scalar_prefetch=1,
            grid=(REACH, CHUNK_PAIRS),
            in_specs=[pl.BlockSpec((rows, PAIR_QUERIES), lambda d, i, n: (0, i))] * REACH
            + [lent_spec, lent_spec]
            + [pl.BlockSpec(memory_space=pl.ANY)] * len(order),
            out_specs=(pl.BlockSpec((rows, CW + LANES), lambda d, i, n: (0, 0)),) * REACH,
            scratch_shapes=[
                pltpu.VMEM((rows, PAIR_QUERIES), jnp.bfloat16),
                pltpu.VMEM((rows, PAIR_QUERIES), jnp.bfloat16),
                pltpu.VMEM((rows, LANES), jnp.float32),
            ],
        ),
        cost_estimate=pl.CostEstimate(
            flops=16 * REACH * rows * lent_rows * CW,
            bytes_accessed=4 * REACH * lent_rows * CHUNK_PAIRS * PAIR_KEYS,
            transcendentals=REACH * rows * CHUNK_HEADS * lent_rows,
        ),
        name="lent",
    )(lent_len, *queries, lent_keys, lent_values, *order)


def local_kernel(
    orders, index_ref, query_ref, cache_key_ref, cache_value_ref, key_ref, value_ref, *refs
):
    out_ref, stat_ref = refs[orders:]
    step = pl.program_id(0)
    rows = query_ref.shape[0]
    cache_rows = cache_key_ref.shape[0]
    own_rows = index_ref[0] * rows

    def mask(part):
        row = lax.broadcasted_iota(jnp.int32, part.shape, 0) % rows
        at = lax.broadcasted_iota(jnp.int32, part.shape, 1)
        valid = (at < own_rows) | ((at >= cache_rows) & (at - cache_rows <= row))
        return jnp.where(valid, part, NEG)

    @pl.when(step == 0)
    def _():
        stat_ref[...] = jnp.zeros_like(stat_ref)

    keys = jnp.concatenate([cache_key_ref[...], key_ref[...]], axis=0)
    values = jnp.concatenate([cache_value_ref[...], value_ref[...]], axis=0)
    stat = stat_ref[...]
    both = attend(query_ref, keys, values, mask)
    for head in range(2):
        out, lse = both[head]
        stat = note_lse(stat, lse, rows, step, head)
        for p in range(GROUP // 2):
            start = head * GROUP * HEAD_SIZE + p * LANES
            out_ref[:, start : start + LANES] = out[p * rows : (p + 1) * rows].astype(
                jnp.bfloat16
            )
    stat_ref[...] = stat


def local_terms(
    part, queries, cache_keys, cache_values, own_keys, own_values, slice_index, order
):
    rows = queries.shape[0]
    cache_rows = cache_keys.shape[0]
    base = part * CHUNK_PAIRS
    query_base = base if queries.shape[1] == QW else 0
    cache_spec = pl.BlockSpec((cache_rows, PAIR_KEYS), lambda i, n: (0, base + i))
    own_spec = pl.BlockSpec((rows, PAIR_KEYS), lambda i, n: (0, base + i))
    return pl.pallas_call(
        functools.partial(local_kernel, len(order)),
        out_shape=(
            jax.ShapeDtypeStruct((rows, CW), jnp.bfloat16),
            jax.ShapeDtypeStruct((rows, LANES), jnp.float32),
        ),
        grid_spec=pltpu.PrefetchScalarGridSpec(
            num_scalar_prefetch=1,
            grid=(CHUNK_PAIRS,),
            in_specs=[
                pl.BlockSpec((rows, PAIR_QUERIES), lambda i, n: (0, query_base + i)),
                cache_spec,
                cache_spec,
                own_spec,
                own_spec,
            ]
            + [pl.BlockSpec(memory_space=pl.ANY)] * len(order),
            out_specs=(
                pl.BlockSpec((rows, PAIR_QUERIES), lambda i, n: (0, i)),
                pl.BlockSpec((rows, LANES), lambda i, n: (0, 0)),
            ),
        ),
        cost_estimate=pl.CostEstimate(
            flops=16 * rows * (cache_rows + rows) * CW,
            bytes_accessed=4 * (cache_rows + rows) * CHUNK_PAIRS * PAIR_KEYS,
            transcendentals=rows * CHUNK_HEADS * (cache_rows + rows),
        ),
        name="local",
    )(slice_index, queries, cache_keys, cache_values, own_keys, own_values, *order)


def spread_dot(left, right):
    high = left.astype(jnp.bfloat16)
    rest = (left - high.astype(jnp.float32)).astype(jnp.bfloat16)
    return jnp.dot(high, right, preferred_element_type=jnp.float32) + jnp.dot(
        rest, right, preferred_element_type=jnp.float32
    )


def combine_kernel(with_next, extra, *refs):
    plan_ref, next_plan_ref, local_ref, local_stat_ref, sink_ref = refs[:5]
    outs = refs[5 : 5 + REACH]
    stats = refs[5 + REACH : 5 + 2 * REACH]
    rest = refs[5 + 2 * REACH :]
    inputs = 2 if with_next else 0
    rest = rest[:inputs] + rest[inputs + extra :]
    step = pl.program_id(0)
    rows, width = local_ref.shape
    halves = rows // QB
    sink = jnp.broadcast_to(sink_ref[...], (rows, LANES))
    lses = [local_stat_ref[...]]
    for d in range(REACH):
        stat = stats[d][...].astype(jnp.float32)
        lse = stat
        for part in range(1, LANES // CHUNK_HEADS):
            lse = lse + pltpu.roll(stat, part * CHUNK_HEADS, 1)
        lses.append(
            jnp.concatenate(
                [jnp.where(plan_ref[d] == half, lse, NEG) for half in range(halves)], axis=0
            )
        )
    top = functools.reduce(jnp.maximum, lses, sink)
    factors = [jnp.exp(lse - top) for lse in lses]
    denom = functools.reduce(lambda a, b: a + b, factors) + jnp.exp(sink - top)
    head_of_row = lax.broadcasted_iota(jnp.int32, (LANES, width), 0) % CHUNK_HEADS
    head_of_lane = lax.broadcasted_iota(jnp.int32, (LANES, width), 1) // HEAD_SIZE
    expand = (head_of_row == head_of_lane + step * (width // HEAD_SIZE)).astype(jnp.bfloat16)
    spread = []
    for factor in factors:
        share = factor / denom
        spread.append(jnp.dot(split_parts(share), expand, preferred_element_type=jnp.float32))
    result = local_ref[...].astype(jnp.float32) * spread[0]
    for d in range(REACH):
        block = outs[d][...].astype(jnp.float32)
        result = result + jnp.concatenate([block] * halves, axis=0) * spread[d + 1]
    rounded = result.astype(jnp.bfloat16)
    if not with_next:
        rest[0][...] = rounded
        return
    query_ref, gain_ref, first_ref, next_ref = rest[:4]
    blocks = rest[4:]
    first_ref[...] = rounded
    stream = query_ref[...].astype(jnp.float32) + rounded.astype(jnp.float32)
    ones = (
        lax.broadcasted_iota(jnp.int32, (LANES, LANES), 0) // HEAD_SIZE
        == lax.broadcasted_iota(jnp.int32, (LANES, LANES), 1) // HEAD_SIZE
    ).astype(jnp.bfloat16)
    square = stream * stream
    sums = jnp.concatenate(
        [
            spread_dot(square[:, c : c + LANES], ones)
            for c in range(0, width, LANES)
        ],
        axis=1,
    )
    scale = lax.rsqrt(sums * (1.0 / HEAD_SIZE) + 1e-06)
    following = ((stream * scale) * gain_ref[...]).astype(jnp.bfloat16)
    next_ref[...] = following
    for d in range(REACH):
        block = following[:QB]
        for half in range(1, halves):
            block = jnp.where(
                next_plan_ref[d] == half, following[half * QB : (half + 1) * QB], block
            )
        blocks[d][...] = block


def combine(part, plan, next_plan, local, returned, sinks, earlier, order, queries=None, gain=None):
    local_out, local_stat = local
    rows = local_out.shape[0]
    width = PAIR_QUERIES
    base = part * CHUNK_PAIRS
    with_next = queries is not None
    here = pl.BlockSpec((rows, width), lambda i, a, b: (0, i))
    wide = pl.BlockSpec((rows, width), lambda i, a, b: (0, base + i))
    block = pl.BlockSpec((QB, width), lambda i, a, b: (0, i))
    in_specs = [
        here,
        pl.BlockSpec((rows, LANES), lambda i, a, b: (0, 0)),
        pl.BlockSpec((1, LANES), lambda i, a, b: (0, part)),
    ]
    in_specs += [block] * REACH
    in_specs += [pl.BlockSpec((QB, LANES), lambda i, a, b: (0, CW // LANES))] * REACH
    args = [local_out, local_stat, sinks, *returned, *returned]
    shape = jax.ShapeDtypeStruct((rows, QW), jnp.bfloat16)
    if with_next:
        in_specs += [wide, pl.BlockSpec((1, width), lambda i, a, b: (0, base + i))]
        args += [queries, gain]
        out_shape = (shape, jax.ShapeDtypeStruct((rows, CW), jnp.bfloat16))
        out_shape += (jax.ShapeDtypeStruct((QB, CW), jnp.bfloat16),) * REACH
        out_specs = (wide, here) + (block,) * REACH
    else:
        out_shape = (shape,)
        out_specs = (wide,)
    extra = list(order)
    aliases = {}
    if earlier is not None:
        extra.append(earlier)
        aliases = {2 + len(args) + len(extra) - 1: 0}
    in_specs += [pl.BlockSpec(memory_space=pl.ANY)] * len(extra)
    return pl.pallas_call(
        functools.partial(combine_kernel, with_next, len(extra)),
        out_shape=out_shape,
        grid_spec=pltpu.PrefetchScalarGridSpec(
            num_scalar_prefetch=2,
            grid=(CW // width,),
            in_specs=in_specs,
            out_specs=out_specs,
        ),
        input_output_aliases=aliases,
        name="combine",
    )(plan, next_plan, *args, *extra)


def body(
    queries,
    slice_keys,
    slice_values,
    cache_keys,
    cache_values,
    lent_keys,
    lent_values,
    lent_len,
    slice_index,
    lend_block,
    sinks,
    gain,
):
    sink_row = jnp.tile(sinks.reshape(CHUNKS, 1, CHUNK_HEADS), (1, LANES // CHUNK_HEADS, 1))
    sink_row = sink_row.reshape(1, CHUNKS * LANES)
    gain_row = gain[None, :]
    first_plan = lend_block[0, 0]
    second_plan = lend_block[1, 0]

    def block_of(part, d):
        rows = lax.dynamic_slice_in_dim(queries, first_plan[d] * QB, QB, 0)
        return rows[:, part * CW : (part + 1) * CW]

    def send(blocks, extra):
        return [from_behind(blocks[d], "section", d + 1 + extra) for d in range(REACH)]

    def lent(part, arrived, order):
        return lent_terms(part, arrived, lent_keys, lent_values, lent_len, order)

    def back(terms):
        return [from_behind(terms[d], "section", -(d + 1)) for d in range(REACH)]

    def local(part, current, own_keys, own_values, order):
        return local_terms(
            part, current, cache_keys, cache_values, own_keys, own_values, slice_index, order
        )

    arrived = [send([block_of(part, d) for d in range(REACH)], 0) for part in range(CHUNKS)]
    next_plan = from_behind(second_plan, "section", -1)
    moved_k = from_behind(slice_keys, "section", 1)
    moved_v = from_behind(slice_values, "section", 1)

    local_0 = local(0, queries, slice_keys, slice_values, [])
    terms_0 = lent(0, arrived[0], [local_0[1]])
    back_0 = back(terms_0)
    terms_1 = lent(1, arrived[1], [terms_0[0], next_plan])
    back_1 = back(terms_1)
    first, follow_0, *blocks_0 = combine(
        0, first_plan, next_plan, local_0, back_0, sink_row, None, [terms_1[0]], queries, gain_row
    )
    next_0 = send(blocks_0, 1)
    moved_0 = from_behind(follow_0, "section", 1)
    local_1 = local(1, queries, slice_keys, slice_values, [follow_0, moved_k, moved_v])
    first, follow_1, *blocks_1 = combine(
        1, first_plan, next_plan, local_1, back_1, sink_row, first, [], queries, gain_row
    )
    next_1 = send(blocks_1, 1)
    moved_1 = from_behind(follow_1, "section", 1)
    terms_0 = lent(0, next_0, [follow_1])
    back_0 = back(terms_0)
    local_0 = local(0, moved_0, moved_k, moved_v, [terms_0[0]])
    terms_1 = lent(1, next_1, [local_0[1]])
    back_1 = back(terms_1)
    (second,) = combine(
        0, second_plan, second_plan, local_0, back_0, sink_row, None, [terms_1[0]]
    )
    local_1 = local(1, moved_1, moved_k, moved_v, [terms_1[0], second])
    (second,) = combine(1, second_plan, second_plan, local_1, back_1, sink_row, second, [])
    return (first, second)


def solution(mesh):
    placed = (
        P(("groups", "section"), None),
        P(("groups", "section"), None),
        P(("groups", "section"), None),
        P(("groups", "section"), None),
        P(("groups", "section"), None),
        P(("groups", "section"), None, None, None),
        P(("groups", "section"), None, None, None),
        P(("groups", "section"), None),
        P(("groups", "section")),
        P(None, ("groups", "section"), None),
        P(),
        P(),
    )
    return jax.shard_map(
        body,
        mesh=mesh,
        in_specs=placed,
        out_specs=(P(("groups", "section"), None), P(("groups", "section"), None)),
        check_vma=False,
    )
```
